32 devices in a mesh: rep: 16 (over z, x, core), fsdp: 2 (over y).
Axes of the slice: x: 2, y: 2, z: 4, core: 2. Of those that a mesh axis runs over, the one named last changes fastest.
Arguments:
- contexts: bfloat16 [16, 256, 2048], P('rep', 'fsdp'), may hold values from -6 to 6
- residual: bfloat16 [16, 256, 4096], P('rep', 'fsdp'), may hold values from -6 to 6
- cotangent: bfloat16 [16, 256, 4096], P('rep', 'fsdp'), may hold values from -96 to 96
- token_ids: int32 [16, 256], P('rep', 'fsdp'), may hold values from 0 to 31999, as said below
- step_index: int32 [1], replicated, may hold values from 0 to 999
- weight: bfloat16 [16, 2048, 4096], P('rep', None, 'fsdp'), may hold values from -0.125 to 0.125
- norm_gain: bfloat16 [16, 4096], P('rep', 'fsdp'), may hold values from 0.5 to 1.5
- momentum: bfloat16 [16, 2048, 4096], P('rep', None, 'fsdp'), may hold values from -6 to 6
- gain_momentum: bfloat16 [16, 4096], P('rep', 'fsdp'), may hold values from -6 to 6
Outputs:
- new_weight: bfloat16 [16, 2048, 4096], P('rep', None, 'fsdp')
- new_gain: bfloat16 [16, 4096], P('rep', 'fsdp')
- new_momentum: bfloat16 [16, 2048, 4096], P('rep', None, 'fsdp')
- new_gain_momentum: bfloat16 [16, 4096], P('rep', 'fsdp')
The draws below stay inside these ranges and needn't reach their ends.
Inputs may be any that keep to these rules, and one draw needn't show every extreme that they name: `token_ids`: ids of 31744 and above are action tokens; the last token of every replica is one.
All inputs are finite; a program needn't handle non-finite values.
Results may differ from the reference program's by a relative error of at most 0.0095.
Values may be sent and summed in bfloat16 or wider, within the bound.
No kernel may reach another device: no remote copies, remote signals or barrier semaphores. Data moves between devices by JAX's collectives and lax.ppermute only.
A program may use at most 128 MiB of HBM per device.

```python
import jax
import jax.numpy as jnp
from jax import lax

D = 4096
HD = 2048
VOCAB = 32000
ACTION = 256
TOKENS = 256
N_REP = 16


def draw_token_ids(key, part):
    keys = jax.random.split(jax.random.fold_in(key, 17), 3)
    position = jnp.arange(TOKENS, dtype=jnp.int32)
    shape = (N_REP, TOKENS)
    chance = 15 + 45 * position // TOKENS
    rolled = jax.random.randint(keys[0], shape, 0, 100)
    action = (rolled < chance[None, :]) | (position[None, :] == TOKENS - 1)
    action_ids = VOCAB - ACTION + jax.random.randint(keys[1], shape, 0, ACTION)
    text_ids = jax.random.randint(keys[2], shape, 0, VOCAB - ACTION)
    return jnp.where(action, action_ids, text_ids).astype(jnp.int32)


def paired_fields(key):
    keys = jax.random.split(jax.random.fold_in(key, 29), 3)
    shape = (N_REP, TOKENS, D)
    base = jnp.clip(jax.random.normal(keys[0], shape, jnp.float32), -6.0, 6.0)
    noise = jax.random.normal(keys[1], shape, jnp.float32)
    share = jax.random.uniform(keys[2], (N_REP, TOKENS, 1), jnp.float32, 0.3, 0.8)
    direction = base * jax.lax.rsqrt(jnp.mean(base * base, axis=-1, keepdims=True) + 1e-06)
    mixed = share * direction + jnp.sqrt(1.0 - share * share) * noise
    cotangent = 16.0 * jnp.clip(mixed, -6.0, 6.0)
    return (base, cotangent)


def draw_residual(key, part):
    base, cotangent = paired_fields(key)
    return base.astype(jnp.bfloat16)


def draw_cotangent(key, part):
    base, cotangent = paired_fields(key)
    return cotangent.astype(jnp.bfloat16)


def block_levels(stream_key, extent, pieces, low, top_value):
    gain = 1.0
    for axis_at, parts in pieces:
        heights = jax.random.uniform(jax.random.fold_in(jax.random.fold_in(stream_key, 6), axis_at), (parts,), jnp.float32, low / len(pieces), top_value / len(pieces))
        gain = gain * jnp.repeat(jnp.exp(heights), extent[axis_at] // parts).reshape((-1,) + (1,) * (len(extent) - 1 - axis_at))
    return gain


def gaussian(rng, extent, width, most, cuts=(), kind=jnp.bfloat16):
    level = block_levels(rng, extent, cuts, -0.22, 0.18) if cuts else 1.0
    result = jax.random.normal(rng, extent, jnp.float32) * width * level
    return jnp.minimum(jnp.maximum(result, -most), most).astype(kind)


def setup_inputs(seed: int = 0) -> dict:
    streams_of = jax.random.split(jax.random.key(seed), 10)
    contexts = gaussian(streams_of[0], (N_REP, TOKENS, HD), 1.0, 6.0, ((0, 16), (1, 2)))
    residual = draw_residual(jax.random.fold_in(streams_of[9], 71), 0)
    cotangent = draw_cotangent(jax.random.fold_in(streams_of[9], 71), 0)
    token_ids = draw_token_ids(jax.random.fold_in(streams_of[9], 71), 0)
    step_index = jax.random.randint(streams_of[4], (1,), 0, 1000).astype(jnp.int32)
    weight = gaussian(streams_of[5], (N_REP, HD, D), HD ** -0.5, 0.125, ((0, 16), (2, 2)))
    norm_gain = jnp.clip(1.0 + 0.1 * jax.random.normal(streams_of[6], (N_REP, D), jnp.float32), 0.5, 1.5).astype(jnp.bfloat16)
    momentum = gaussian(streams_of[7], (N_REP, HD, D), 1.0, 6.0, ((0, 16), (2, 2)))
    gain_momentum = gaussian(streams_of[8], (N_REP, D), 1.0, 6.0, ((0, 16), (1, 2)))
    return {"contexts": contexts, "residual": residual, "cotangent": cotangent, "token_ids": token_ids, "step_index": step_index, "weight": weight, "norm_gain": norm_gain, "momentum": momentum, "gain_momentum": gain_momentum}


EPSILON = 1e-05
BETA = 0.9
LEARN_RATE = 0.05

def replica_update(items):
    contexts, residual, cotangent, token_ids, weight, norm_gain, momentum, gain_momentum = items
    pre = residual.astype(jnp.float32) + jnp.dot(contexts, weight, preferred_element_type=jnp.float32)
    inv = lax.rsqrt(lax.optimization_barrier(jnp.mean(pre * pre, axis=-1, keepdims=True)) + EPSILON)
    normed = pre * inv
    mask = (token_ids >= VOCAB - ACTION).astype(jnp.float32)
    count = jnp.sum(mask)
    scaled = cotangent.astype(jnp.float32) * mask[:, None] / count
    weighted = scaled * norm_gain.astype(jnp.float32)[None, :]
    inner = lax.optimization_barrier(jnp.mean(weighted * normed, axis=-1, keepdims=True))
    grad_pre = (inv * (weighted - normed * inner)).astype(jnp.bfloat16)
    grad_weight = lax.dot_general(contexts, grad_pre, (((0,), (0,)), ((), ())), preferred_element_type=jnp.float32)
    grad_gain = lax.optimization_barrier(jnp.sum(scaled * normed, axis=0))
    mom_w = (BETA * momentum.astype(jnp.float32) + grad_weight).astype(jnp.bfloat16)
    mom_g = (BETA * gain_momentum.astype(jnp.float32) + grad_gain).astype(jnp.bfloat16)
    mom_w = lax.optimization_barrier(mom_w)
    mom_g = lax.optimization_barrier(mom_g)
    par_w = (weight.astype(jnp.float32) - LEARN_RATE * mom_w.astype(jnp.float32)).astype(jnp.bfloat16)
    par_g = (norm_gain.astype(jnp.float32) - LEARN_RATE * mom_g.astype(jnp.float32)).astype(jnp.bfloat16)
    return (par_w, par_g, mom_w, mom_g)

def average_pair(values, distance):
    return tuple((((item.astype(jnp.float32) + jnp.roll(item, distance, axis=0).astype(jnp.float32)) * 0.5).astype(jnp.bfloat16) for item in values))

def reference(contexts, residual, cotangent, token_ids, step_index, weight, norm_gain, momentum, gain_momentum):
    updated = lax.map(replica_update, (contexts, residual, cotangent, token_ids, weight, norm_gain, momentum, gain_momentum))
    levels = int(N_REP).bit_length() - 1
    level = step_index[0] % levels
    distance = jnp.left_shift(jnp.int32(1), level.astype(jnp.int32))
    par_w, par_g, mom_w, mom_g = average_pair(updated, distance)
    return (par_w, par_g, mom_w, mom_g)
```

```python
import functools

import jax
import jax.numpy as jnp
from jax import lax
from jax.experimental import pallas as pl
from jax.experimental.pallas import tpu as pltpu
from jax.sharding import PartitionSpec as P

VOCAB = 32000
ACTION = 256


EPSILON = 1e-05
BETA = 0.9
LEARN_RATE = 0.05


SHARES = (4, 4, 4, 2, 1, 1)


def passed_along(array, axis, by):
    peers = lax.axis_size(axis)
    return lax.ppermute(array, axis, [(i, (i + by) % peers) for i in range(peers)])


def momentum_rows_kernel(ctx_ref, grad_ref, momentum_ref, out_ref):
    grad_weight = jnp.dot(ctx_ref[...], grad_ref[...], preferred_element_type=jnp.float32)
    out_ref[...] = (BETA * momentum_ref[...].astype(jnp.float32) + grad_weight).astype(jnp.bfloat16)


def momentum_rows(ctx_t, grad_pre, momentum, first, rows, block):
    tokens, columns = grad_pre.shape
    skip = first // block
    return pl.pallas_call(
        momentum_rows_kernel,
        grid=(rows // block,),
        in_specs=[
            pl.BlockSpec((block, tokens), lambda i: (skip + i, 0)),
            pl.BlockSpec((tokens, columns), lambda i: (0, 0)),
            pl.BlockSpec((None, block, columns), lambda i: (0, skip + i, 0)),
        ],
        out_specs=pl.BlockSpec((block, columns), lambda i: (i, 0)),
        out_shape=jax.ShapeDtypeStruct((rows, columns), jnp.bfloat16),
        cost_estimate=pl.CostEstimate(
            flops=2 * rows * tokens * columns,
            bytes_accessed=4 * rows * columns + 2 * tokens * (rows + columns),
            transcendentals=0,
        ),
    )(ctx_t, grad_pre, momentum)


def average_rows_kernel(weight_ref, far_weight_ref, mom_ref, far_mom_ref, *refs):
    out_weight_ref, out_mom_ref = refs[-2:]
    mom = mom_ref[...].astype(jnp.float32)
    far_mom = far_mom_ref[...].astype(jnp.float32)
    par = weight_ref[...].astype(jnp.float32) - LEARN_RATE * mom
    far_par = far_weight_ref[...].astype(jnp.float32) - LEARN_RATE * far_mom
    par = par.astype(jnp.bfloat16).astype(jnp.float32)
    far_par = far_par.astype(jnp.bfloat16).astype(jnp.float32)
    out_weight_ref[...] = ((par + far_par) * 0.5).astype(jnp.bfloat16)
    out_mom_ref[...] = ((mom + far_mom) * 0.5).astype(jnp.bfloat16)


def average_rows(weight, far_weight, mom, far_mom, held, first, block):
    rows, columns = mom.shape
    skip = first // block
    whole = pl.BlockSpec((None, block, columns), lambda i: (0, skip + i, 0))
    chunk = pl.BlockSpec((block, columns), lambda i: (i, 0))
    shape = jax.ShapeDtypeStruct(weight.shape, jnp.bfloat16)
    return pl.pallas_call(
        average_rows_kernel,
        grid=(rows // block,),
        in_specs=[whole, whole, chunk, chunk] + [pl.BlockSpec(memory_space=pl.ANY)] * len(held),
        out_specs=[whole, whole],
        out_shape=[shape, shape],
        input_output_aliases={4 + at: at for at in range(len(held))},
        cost_estimate=pl.CostEstimate(
            flops=8 * rows * columns, bytes_accessed=12 * rows * columns, transcendentals=0
        ),
    )(weight, far_weight, mom, far_mom, *held)


def row_chunks(rows):
    unit = rows // sum(SHARES)
    first, chunks = 0, []
    for share in SHARES:
        chunks.append((first, share * unit))
        first += share * unit
    return chunks


def replica_step(
    contexts,
    residual,
    cotangent,
    token_ids,
    weight,
    norm_gain,
    momentum,
    gain_momentum,
    me,
    *,
    distance,
):
    peers = lax.axis_size("fsdp")
    hidden, columns = weight.shape[1:]
    width = columns * peers

    far_weight = passed_along(weight, "rep", distance)

    def from_all(block_for, by_shift=passed_along):
        parts = [block_for(me)]
        for shift in range(1, peers):
            parts.append(by_shift(block_for((me + shift) % peers), "fsdp", shift))
        return parts

    def columns_of(array):
        return lambda peer: lax.dynamic_slice_in_dim(array[0], peer * columns, columns, 1)

    ids = jnp.concatenate(from_all(lambda peer: token_ids[0]))
    ctx = jnp.concatenate(from_all(lambda peer: contexts[0]))
    resid = jnp.concatenate(from_all(columns_of(residual)))
    cotan = jnp.concatenate(from_all(columns_of(cotangent)))

    mask = (ids >= VOCAB - ACTION).astype(jnp.float32)
    count = jnp.sum(mask)
    gain = norm_gain[0].astype(jnp.float32)
    pre = resid.astype(jnp.float32) + jnp.dot(ctx, weight[0], preferred_element_type=jnp.float32)
    scaled = cotan.astype(jnp.float32) * mask[:, None] / count
    weighted = scaled * gain[None, :]
    sums = jnp.stack([jnp.sum(pre * pre, axis=-1), jnp.sum(weighted * pre, axis=-1)])
    total = sums
    for shift in range(1, peers):
        total = total + passed_along(jnp.roll(sums, shift * contexts.shape[1], 1), "fsdp", shift)
    inverse = lax.rsqrt(total[0] / width + EPSILON)[:, None]
    inner = inverse * total[1][:, None] / width
    normed = pre * inverse
    grad_pre = (inverse * (weighted - normed * inner)).astype(jnp.bfloat16)
    grad_gain = jnp.sum(scaled * normed, axis=0)

    mom_g = (BETA * gain_momentum[0].astype(jnp.float32) + grad_gain).astype(jnp.bfloat16)
    par_g = (gain - LEARN_RATE * mom_g.astype(jnp.float32)).astype(jnp.bfloat16)
    gains = jnp.stack([par_g, mom_g])
    far_gains = passed_along(gains, "rep", distance)
    new_gains = ((gains.astype(jnp.float32) + far_gains.astype(jnp.float32)) * 0.5).astype(
        jnp.bfloat16
    )

    chunks = row_chunks(hidden)
    block = min(rows for _, rows in chunks)
    ctx_t = ctx.T
    moms = [momentum_rows(ctx_t, grad_pre, momentum, first, rows, block) for first, rows in chunks]
    far_moms = [passed_along(mom, "rep", distance) for mom in moms]
    held = ()
    for (first, _), mom, far_mom in zip(chunks, moms, far_moms):
        held = average_rows(weight, far_weight, mom, far_mom, held, first, block)
    new_weight, new_momentum = held
    return new_weight, new_gains[:1], new_momentum, new_gains[1:]


def shards(
    contexts, residual, cotangent, token_ids, step_index, weight, norm_gain, momentum, gain_momentum
):
    levels = lax.axis_size("rep").bit_length() - 1
    branches = [functools.partial(replica_step, distance=1 << level) for level in range(levels)]
    return lax.switch(
        step_index[0] % levels,
        branches,
        contexts,
        residual,
        cotangent,
        token_ids,
        weight,
        norm_gain,
        momentum,
        gain_momentum,
        lax.axis_index("fsdp"),
    )


def solution(mesh):
    placed = (
        P("rep", "fsdp", None),
        P("rep", "fsdp", None),
        P("rep", "fsdp", None),
        P("rep", "fsdp"),
        P(),
        P("rep", None, "fsdp"),
        P("rep", "fsdp"),
        P("rep", None, "fsdp"),
        P("rep", "fsdp"),
    )
    return jax.shard_map(
        shards,
        mesh=mesh,
        in_specs=placed,
        out_specs=(
            P("rep", None, "fsdp"),
            P("rep", "fsdp"),
            P("rep", None, "fsdp"),
            P("rep", "fsdp"),
        ),
        check_vma=False,
    )
```

```python
import functools

import jax
import jax.numpy as jnp
from jax import lax
from jax.experimental import pallas as pl
from jax.experimental.pallas import tpu as pltpu
from jax.sharding import PartitionSpec as P

VOCAB = 32000
ACTION = 256


EPSILON = 1e-05
BETA = 0.9
LEARN_RATE = 0.05


SHARES = (11, 4, 1)
LANES = 128
TILE = 16


def passed_along(array, axis, by):
    peers = lax.axis_size(axis)
    return lax.ppermute(array, axis, [(i, (i + by) % peers) for i in range(peers)])


def cost(flops, *arrays):
    moved = sum(array.size * array.dtype.itemsize for array in arrays)
    return pl.CostEstimate(flops=flops, bytes_accessed=moved, transcendentals=0)


def largest_block(size, most):
    return max(block for block in range(1, most + 1) if size % block == 0)


def forward_kernel(count_ref, ctx_ref, weight_ref, resid_ref, cotan_ref, gain_ref, pre_ref, sums_ref):
    tokens, columns = resid_ref.shape
    strip = largest_block(tokens, 128)
    at = pl.program_id(0)
    lane = lax.broadcasted_iota(jnp.int32, (strip, LANES), 1)

    @pl.when(at == 0)
    def _():
        sums_ref[...] = jnp.where(
            lax.broadcasted_iota(jnp.int32, sums_ref.shape, 1) == 2, count_ref[0], 0.0
        )

    def one_strip(i, carry):
        rows = pl.ds(pl.multiple_of(i * strip, strip), strip)
        pre = resid_ref[rows, :].astype(jnp.float32) + jnp.dot(
            ctx_ref[rows, :], weight_ref[...], preferred_element_type=jnp.float32
        )
        pre_ref[rows, :] = pre
        weighted = cotan_ref[rows, :].astype(jnp.float32) * gain_ref[...].astype(jnp.float32)
        square = jnp.sum(pre * pre, axis=1, keepdims=True)
        inner = jnp.sum(weighted * pre, axis=1, keepdims=True)
        sums_ref[rows, :] += jnp.where(lane == 0, square, jnp.where(lane == 1, inner, 0.0))
        return carry

    lax.fori_loop(0, tokens // strip, one_strip, 0)


def forward(own_count, ctx, weight, resid, cotan, gain):
    tokens, columns = resid.shape
    hidden = ctx.shape[1]
    block = largest_block(columns, 256)
    out = [
        jax.ShapeDtypeStruct((tokens, columns), jnp.float32),
        jax.ShapeDtypeStruct((tokens, LANES), jnp.float32),
    ]
    by_columns = pl.BlockSpec((tokens, block), lambda i: (0, i))
    return pl.pallas_call(
        forward_kernel,
        grid=(columns // block,),
        in_specs=[
            pl.BlockSpec(memory_space=pltpu.SMEM),
            pl.BlockSpec((tokens, hidden), lambda i: (0, 0)),
            pl.BlockSpec((None, hidden, block), lambda i: (0, 0, i)),
            by_columns,
            by_columns,
            pl.BlockSpec((1, block), lambda i: (0, i)),
        ],
        out_specs=[by_columns, pl.BlockSpec((tokens, LANES), lambda i: (0, 0))],
        out_shape=out,
        cost_estimate=cost(2 * tokens * hidden * columns, ctx, weight, resid, cotan, *out),
        name="forward",
    )(own_count, ctx, weight, resid, cotan, gain)


def gradient_kernel(
    width, pre_ref, cotan_ref, sums_ref, gain_ref, gain_momentum_ref, grad_ref, gains_ref
):
    tokens, columns = pre_ref.shape
    strip = largest_block(tokens, 32)
    gain = gain_ref[...].astype(jnp.float32)

    def one_strip(i, grad_gain):
        rows = pl.ds(pl.multiple_of(i * strip, strip), strip)
        count = sums_ref[rows, 2:3]
        inverse = lax.rsqrt(sums_ref[rows, 0:1] / width + EPSILON)
        inner = inverse * (sums_ref[rows, 1:2] / count) / width
        normed = pre_ref[rows, :] * inverse
        scaled = cotan_ref[rows, :].astype(jnp.float32) / count
        grad = inverse * (scaled * gain - normed * inner)
        grad_ref[rows, :] = grad.astype(jnp.bfloat16)
        return grad_gain + jnp.sum((scaled * normed).reshape(strip // 8, 8, columns), axis=0)

    grad_gain = lax.fori_loop(
        0, tokens // strip, one_strip, jnp.zeros((8, columns), jnp.float32)
    )
    grad_gain = jnp.sum(grad_gain, axis=0, keepdims=True)
    mom = (BETA * gain_momentum_ref[...].astype(jnp.float32) + grad_gain).astype(jnp.bfloat16)
    mom = mom.astype(jnp.float32)
    par = (gain - LEARN_RATE * mom).astype(jnp.bfloat16).astype(jnp.float32)
    row = lax.broadcasted_iota(jnp.int32, (TILE, columns), 0)
    gains_ref[...] = jnp.where(row == 0, par, jnp.where(row == 1, mom, 0.0)).astype(jnp.bfloat16)


def gradient(width, pre, cotan, sums, gain, gain_momentum):
    tokens, columns = pre.shape
    block = largest_block(columns, 256)
    out = [
        jax.ShapeDtypeStruct((tokens, columns), jnp.bfloat16),
        jax.ShapeDtypeStruct((TILE, columns), jnp.bfloat16),
    ]
    by_columns = pl.BlockSpec((tokens, block), lambda i: (0, i))
    one_row = pl.BlockSpec((1, block), lambda i: (0, i))
    return pl.pallas_call(
        functools.partial(gradient_kernel, width),
        grid=(columns // block,),
        in_specs=[
            by_columns,
            by_columns,
            pl.BlockSpec((tokens, LANES), lambda i: (0, 0)),
            one_row,
            one_row,
        ],
        out_specs=[by_columns, pl.BlockSpec((TILE, block), lambda i: (0, i))],
        out_shape=out,
        cost_estimate=cost(12 * tokens * columns, pre, cotan, sums, *out),
        name="gradient",
    )(pre, cotan, sums, gain, gain_momentum)


def momentum_rows_kernel(ctx_ref, grad_ref, momentum_ref, *refs):
    out_ref = refs[-1]
    rows, columns = momentum_ref.shape
    part = largest_block(columns, 512)

    def one_part(i, carry):
        at = pl.ds(pl.multiple_of(i * part, part), part)
        grad_weight = jnp.dot(ctx_ref[...], grad_ref[:, at], preferred_element_type=jnp.float32)
        mom = BETA * momentum_ref[:, at].astype(jnp.float32) + grad_weight
        out_ref[pl.ds(0, rows), at] = mom.astype(jnp.bfloat16)
        return carry

    lax.fori_loop(0, columns // part, one_part, 0)
    if len(refs) == 2:
        out_ref[pl.ds(rows, TILE), :] = refs[0][...]


def momentum_rows(ctx_t, grad_pre, momentum, first, rows, block, gains=None):
    tokens, columns = grad_pre.shape
    skip = first // block
    extra, tail = ([], 0) if gains is None else ([gains], TILE)
    assert gains is None or rows == block
    return pl.pallas_call(
        momentum_rows_kernel,
        grid=(rows // block,),
        in_specs=[
            pl.BlockSpec((block, tokens), lambda i: (skip + i, 0)),
            pl.BlockSpec((tokens, columns), lambda i: (0, 0)),
            pl.BlockSpec((None, block, columns), lambda i: (0, skip + i, 0)),
        ]
        + [pl.BlockSpec((TILE, columns), lambda i: (0, 0)) for _ in extra],
        out_specs=pl.BlockSpec((block + tail, columns), lambda i: (i, 0)),
        out_shape=jax.ShapeDtypeStruct((rows + tail, columns), jnp.bfloat16),
        cost_estimate=pl.CostEstimate(
            flops=2 * rows * tokens * columns,
            bytes_accessed=4 * rows * columns + 2 * tokens * (rows + columns),
            transcendentals=0,
        ),
        name="momentum_rows",
    )(ctx_t, grad_pre, momentum, *extra)


def average_rows_kernel(held, with_gains, *refs):
    weight_ref, far_weight_ref, mom_ref, far_mom_ref = refs[:4]
    outs = refs[4 + held :]
    rows, columns = weight_ref.shape
    part = largest_block(columns, 512)
    parts = columns // part

    def one_part(i, carry):
        here = pl.ds(pl.multiple_of(i // parts * TILE, TILE), TILE)
        at = (here, pl.ds(pl.multiple_of(i % parts * part, part), part))
        mom = mom_ref[at].astype(jnp.float32)
        far_mom = far_mom_ref[at].astype(jnp.float32)
        par = weight_ref[at].astype(jnp.float32) - LEARN_RATE * mom
        far_par = far_weight_ref[at].astype(jnp.float32) - LEARN_RATE * far_mom
        par = par.astype(jnp.bfloat16).astype(jnp.float32)
        far_par = far_par.astype(jnp.bfloat16).astype(jnp.float32)
        outs[0][at] = ((par + far_par) * 0.5).astype(jnp.bfloat16)
        outs[1][at] = ((mom + far_mom) * 0.5).astype(jnp.bfloat16)
        return carry

    lax.fori_loop(0, rows // TILE * parts, one_part, 0)
    if with_gains:
        tile = pl.ds(rows, TILE)
        gains = mom_ref[tile, :].astype(jnp.float32) + far_mom_ref[tile, :].astype(jnp.float32)
        gains = gains * 0.5
        outs[2][...] = gains[0:1].astype(jnp.bfloat16)
        outs[3][...] = gains[1:2].astype(jnp.bfloat16)


def average_rows(weight, far_weight, mom, far_mom, held, first, rows, block):
    columns = mom.shape[1]
    skip, tail = first // block, mom.shape[0] - rows
    whole = pl.BlockSpec((None, block, columns), lambda i: (0, skip + i, 0))
    chunk = pl.BlockSpec((block + tail, columns), lambda i: (i, 0))
    shape = jax.ShapeDtypeStruct(weight.shape, jnp.bfloat16)
    gain_shape = [jax.ShapeDtypeStruct((1, columns), jnp.bfloat16)] * 2 if tail else []
    gain_specs = [pl.BlockSpec((1, columns), lambda i: (0, 0))] * len(gain_shape)
    return pl.pallas_call(
        functools.partial(average_rows_kernel, len(held), bool(tail)),
        grid=(rows // block,),
        in_specs=[whole, whole, chunk, chunk] + [pl.BlockSpec(memory_space=pl.ANY)] * len(held),
        out_specs=[whole, whole] + gain_specs,
        out_shape=[shape, shape] + gain_shape,
        input_output_aliases={4 + at: at for at in range(len(held))},
        cost_estimate=pl.CostEstimate(
            flops=8 * rows * columns, bytes_accessed=12 * rows * columns, transcendentals=0
        ),
        name="average_rows",
    )(weight, far_weight, mom, far_mom, *held)


def replica_step(
    contexts,
    residual,
    cotangent,
    token_ids,
    weight,
    norm_gain,
    momentum,
    gain_momentum,
    me,
    *,
    distance,
):
    peers = lax.axis_size("fsdp")
    tokens = contexts.shape[1]
    hidden, columns = weight.shape[1:]

    far_weight = passed_along(weight, "rep", distance)

    def from_all(block_for):
        parts = [block_for(me)]
        for shift in range(1, peers):
            parts.append(passed_along(block_for((me + shift) % peers), "fsdp", shift))
        return jnp.concatenate(parts)

    def columns_of(array):
        return lambda peer: lax.dynamic_slice_in_dim(array, peer * columns, columns, 1)

    action = token_ids[0] >= VOCAB - ACTION
    own_count = jnp.sum(action.astype(jnp.float32)).reshape(1)
    masked = jnp.where(action[:, None], cotangent[0], jnp.zeros((), cotangent.dtype))
    ctx = from_all(lambda peer: contexts[0])
    resid = from_all(columns_of(residual[0]))
    cotan = from_all(columns_of(masked))

    pre, sums = forward(own_count, ctx, weight, resid, cotan, norm_gain)
    total = sums
    for shift in range(1, peers):
        total = total + jnp.roll(passed_along(sums, "fsdp", shift), shift * tokens, 0)
    grad_pre, gains = gradient(columns * peers, pre, cotan, total, norm_gain, gain_momentum)

    unit = hidden // sum(SHARES)
    ctx_t = ctx.T
    first, held = 0, ()
    for share in SHARES:
        rows = share * unit
        last = first + rows == hidden
        mom = momentum_rows(ctx_t, grad_pre, momentum, first, rows, unit, gains if last else None)
        far_mom = passed_along(mom, "rep", distance)
        held = average_rows(weight, far_weight, mom, far_mom, held[:2], first, rows, unit)
        first += rows
    new_weight, new_momentum, new_gain, new_gain_momentum = held
    return new_weight, new_gain, new_momentum, new_gain_momentum


def shards(
    contexts, residual, cotangent, token_ids, step_index, weight, norm_gain, momentum, gain_momentum
):
    levels = lax.axis_size("rep").bit_length() - 1
    branches = [functools.partial(replica_step, distance=1 << level) for level in range(levels)]
    return lax.switch(
        step_index[0] % levels,
        branches,
        contexts,
        residual,
        cotangent,
        token_ids,
        weight,
        norm_gain,
        momentum,
        gain_momentum,
        lax.axis_index("fsdp"),
    )


def solution(mesh):
    placed = (
        P("rep", "fsdp", None),
        P("rep", "fsdp", None),
        P("rep", "fsdp", None),
        P("rep", "fsdp"),
        P(),
        P("rep", None, "fsdp"),
        P("rep", "fsdp"),
        P("rep", None, "fsdp"),
        P("rep", "fsdp"),
    )
    return jax.shard_map(
        shards,
        mesh=mesh,
        in_specs=placed,
        out_specs=(
            P("rep", None, "fsdp"),
            P("rep", "fsdp"),
            P("rep", None, "fsdp"),
            P("rep", "fsdp"),
        ),
        check_vma=False,
    )
```

```python
import functools
import math

import jax
import jax.numpy as jnp
from jax import lax
from jax.experimental import pallas as pl
from jax.experimental.pallas import tpu as pltpu
from jax.sharding import PartitionSpec as P

VOCAB = 32000
ACTION = 256


EPSILON = 1e-05
BETA = 0.9
LEARN_RATE = 0.05


SHARES = (11, 3, 1, 1)
LANES = 128
TILE = 16


def passed_along(array, axis, by):
    peers = lax.axis_size(axis)
    return lax.ppermute(array, axis, [(i, (i + by) % peers) for i in range(peers)])


def cost(flops, *arrays):
    moved = sum(array.size * array.dtype.itemsize for array in arrays)
    return pl.CostEstimate(flops=flops, bytes_accessed=moved, transcendentals=0)


def vmem(*blocks):
    room = sum(2 * size * math.prod(shape) for shape, size in blocks) + 3 * 2**20
    return pltpu.CompilerParams(vmem_limit_bytes=room)


def largest_block(size, most):
    return max(block for block in range(1, most + 1) if size % block == 0)


def forward_kernel(count_ref, ctx_ref, weight_ref, resid_ref, cotan_ref, gain_ref, pre_ref, sums_ref):
    tokens, _ = resid_ref.shape
    strip = largest_block(tokens, 128)
    at = pl.program_id(0)
    lane = lax.broadcasted_iota(jnp.int32, (strip, LANES), 1)

    @pl.when(at == 0)
    def _():
        sums_ref[...] = jnp.where(
            lax.broadcasted_iota(jnp.int32, sums_ref.shape, 1) == 2, count_ref[0], 0.0
        )

    def one_strip(i, carry):
        rows = pl.ds(pl.multiple_of(i * strip, strip), strip)
        pre = resid_ref[rows, :].astype(jnp.float32) + jnp.dot(
            ctx_ref[rows, :], weight_ref[...], preferred_element_type=jnp.float32
        )
        pre_ref[rows, :] = pre
        weighted = cotan_ref[rows, :].astype(jnp.float32) * gain_ref[...].astype(jnp.float32)
        square = jnp.sum(pre * pre, axis=1, keepdims=True)
        inner = jnp.sum(weighted * pre, axis=1, keepdims=True)
        sums_ref[rows, :] += jnp.where(lane == 0, square, jnp.where(lane == 1, inner, 0.0))
        return carry

    lax.fori_loop(0, tokens // strip, one_strip, 0)


def forward(own_count, ctx, weight, resid, cotan, gain):
    tokens, columns = resid.shape
    hidden = ctx.shape[1]
    block = largest_block(columns, 256)
    out = [
        jax.ShapeDtypeStruct((tokens, columns), jnp.float32),
        jax.ShapeDtypeStruct((tokens, LANES), jnp.float32),
    ]
    by_columns = pl.BlockSpec((tokens, block), lambda i: (0, i))
    return pl.pallas_call(
        forward_kernel,
        grid=(columns // block,),
        in_specs=[
            pl.BlockSpec(memory_space=pltpu.SMEM),
            pl.BlockSpec((tokens, hidden), lambda i: (0, 0)),
            pl.BlockSpec((None, hidden, block), lambda i: (0, 0, i)),
            by_columns,
            by_columns,
            pl.BlockSpec((1, block), lambda i: (0, i)),
        ],
        out_specs=[by_columns, pl.BlockSpec((tokens, LANES), lambda i: (0, 0))],
        out_shape=out,
        compiler_params=vmem(
            ((tokens, hidden), 2), ((hidden, block), 2), ((tokens, block), 8), ((tokens, LANES), 4)
        ),
        cost_estimate=cost(2 * tokens * hidden * columns, ctx, weight, resid, cotan, *out),
        name="forward",
    )(own_count, ctx, weight, resid, cotan, gain)


def gradient_kernel(
    width, pre_ref, cotan_ref, sums_ref, gain_ref, gain_momentum_ref, grad_ref, gains_ref
):
    tokens, columns = pre_ref.shape
    gain = gain_ref[...].astype(jnp.float32)

    def one_strip(i, grad_gain):
        rows = pl.ds(pl.multiple_of(i * TILE, TILE), TILE)
        inverse = lax.rsqrt(sums_ref[rows, 0:1] / width + EPSILON)
        share = 1.0 / sums_ref[rows, 2:3]
        inner = inverse * (sums_ref[rows, 1:2] * share) / width
        normed = pre_ref[rows, :] * inverse
        scaled = cotan_ref[rows, :].astype(jnp.float32) * share
        grad = inverse * (scaled * gain - normed * inner)
        grad_ref[rows, :] = grad.astype(jnp.bfloat16)
        product = scaled * normed
        return grad_gain + (product[: TILE // 2] + product[TILE // 2 :])

    grad_gain = lax.fori_loop(
        0, tokens // TILE, one_strip, jnp.zeros((TILE // 2, columns), jnp.float32)
    )
    grad_gain = jnp.sum(grad_gain, axis=0, keepdims=True)
    mom = (BETA * gain_momentum_ref[...].astype(jnp.float32) + grad_gain).astype(jnp.bfloat16)
    mom = mom.astype(jnp.float32)
    par = (gain - LEARN_RATE * mom).astype(jnp.bfloat16).astype(jnp.float32)
    row = lax.broadcasted_iota(jnp.int32, gains_ref.shape, 0)
    gains_ref[...] = jnp.where(row == 0, par, mom).astype(jnp.bfloat16)


def gradient(width, pre, cotan, sums, gain, gain_momentum):
    tokens, columns = pre.shape
    block = largest_block(columns, 1024)
    out = [
        jax.ShapeDtypeStruct((tokens, columns), jnp.bfloat16),
        jax.ShapeDtypeStruct((2, columns), jnp.bfloat16),
    ]
    by_columns = pl.BlockSpec((tokens, block), lambda i: (0, i))
    one_row = pl.BlockSpec((1, block), lambda i: (0, i))
    return pl.pallas_call(
        functools.partial(gradient_kernel, width),
        grid=(columns // block,),
        in_specs=[
            by_columns,
            by_columns,
            pl.BlockSpec((tokens, LANES), lambda i: (0, 0)),
            one_row,
            one_row,
        ],
        out_specs=[by_columns, pl.BlockSpec((2, block), lambda i: (0, i))],
        out_shape=out,
        compiler_params=vmem(((tokens, block), 8), ((tokens, LANES), 4), ((8, block), 6)),
        cost_estimate=cost(12 * tokens * columns, pre, cotan, sums, *out),
        name="gradient",
    )(pre, cotan, sums, gain, gain_momentum)


def momentum_rows_kernel(ctx_ref, grad_ref, momentum_ref, out_ref):
    columns = momentum_ref.shape[1]
    part = largest_block(columns, 512)

    def one_part(i, carry):
        at = pl.ds(pl.multiple_of(i * part, part), part)
        grad_weight = jnp.dot(ctx_ref[...], grad_ref[:, at], preferred_element_type=jnp.float32)
        mom = BETA * momentum_ref[:, at].astype(jnp.float32) + grad_weight
        out_ref[:, at] = mom.astype(jnp.bfloat16)
        return carry

    lax.fori_loop(0, columns // part, one_part, 0)


def momentum_rows(ctx_t, grad_pre, momentum, first, rows, block):
    tokens, columns = grad_pre.shape
    skip = first // block
    return pl.pallas_call(
        momentum_rows_kernel,
        grid=(rows // block,),
        in_specs=[
            pl.BlockSpec((block, tokens), lambda i: (skip + i, 0)),
            pl.BlockSpec((tokens, columns), lambda i: (0, 0)),
            pl.BlockSpec((None, block, columns), lambda i: (0, skip + i, 0)),
        ],
        out_specs=pl.BlockSpec((block, columns), lambda i: (i, 0)),
        out_shape=jax.ShapeDtypeStruct((rows, columns), jnp.bfloat16),
        compiler_params=vmem(((block, tokens), 2), ((tokens, columns), 2), ((block, columns), 4)),
        cost_estimate=pl.CostEstimate(
            flops=2 * rows * tokens * columns,
            bytes_accessed=4 * rows * columns + 2 * tokens * (rows + columns),
            transcendentals=0,
        ),
        name="momentum_rows",
    )(ctx_t, grad_pre, momentum)


def average_block(weight_ref, far_weight_ref, mom_ref, far_mom_ref, out_weight_ref, out_mom_ref, first=0):
    rows, columns = out_weight_ref.shape
    part = largest_block(columns, 512)
    parts = columns // part

    def one_part(i, carry):
        row = i // parts * TILE
        column = pl.ds(pl.multiple_of(i % parts * part, part), part)
        out = (pl.ds(pl.multiple_of(row, TILE), TILE), column)
        at = (pl.ds(pl.multiple_of(first + row, TILE), TILE), column)
        mom = mom_ref[at].astype(jnp.float32)
        far_mom = far_mom_ref[at].astype(jnp.float32)
        par = weight_ref[at].astype(jnp.float32) - LEARN_RATE * mom
        far_par = far_weight_ref[at].astype(jnp.float32) - LEARN_RATE * far_mom
        par = par.astype(jnp.bfloat16).astype(jnp.float32)
        far_par = far_par.astype(jnp.bfloat16).astype(jnp.float32)
        out_weight_ref[out] = ((par + far_par) * 0.5).astype(jnp.bfloat16)
        out_mom_ref[out] = ((mom + far_mom) * 0.5).astype(jnp.bfloat16)
        return carry

    lax.fori_loop(0, rows // TILE * parts, one_part, 0)


def average_rows_kernel(weight_ref, far_weight_ref, mom_ref, far_mom_ref, *refs):
    average_block(weight_ref, far_weight_ref, mom_ref, far_mom_ref, *refs[-2:])


def average_cost(rows, columns):
    return pl.CostEstimate(
        flops=8 * rows * columns, bytes_accessed=12 * rows * columns, transcendentals=0
    )


def average_rows(weight, far_weight, mom, far_mom, held, first, block):
    rows, columns = mom.shape
    skip = first // block
    whole = pl.BlockSpec((None, block, columns), lambda i: (0, skip + i, 0))
    chunk = pl.BlockSpec((block, columns), lambda i: (i, 0))
    shape = pltpu.HBM(weight.shape, jnp.bfloat16)
    return pl.pallas_call(
        average_rows_kernel,
        grid=(rows // block,),
        in_specs=[whole, whole, chunk, chunk] + [pl.BlockSpec(memory_space=pl.ANY)] * len(held),
        out_specs=[whole, whole],
        out_shape=[shape, shape],
        input_output_aliases={4 + at: at for at in range(len(held))},
        compiler_params=vmem(((block, columns), 12)),
        cost_estimate=average_cost(rows, columns),
        name="average_rows",
    )(weight, far_weight, mom, far_mom, *held)


def average_last_kernel(
    weight_ref, far_weight_ref, mom_ref, far_mom_ref, gains_ref, far_gains_ref, *refs
):
    out_weight_ref, out_mom_ref, out_gain_ref, out_gain_mom_ref = refs[-4:]
    first = pl.program_id(0) * out_weight_ref.shape[0]
    average_block(
        weight_ref, far_weight_ref, mom_ref, far_mom_ref, out_weight_ref, out_mom_ref, first
    )

    @pl.when(first == 0)
    def _():
        gains = gains_ref[...].astype(jnp.float32) + far_gains_ref[...].astype(jnp.float32)
        gains = (gains * 0.5).astype(jnp.bfloat16)
        out_gain_ref[...] = gains[0:1]
        out_gain_mom_ref[...] = gains[1:2]


def average_last(weight, far_weight, mom, far_mom, gains, far_gains, held, first):
    rows, columns = mom.shape
    block = largest_block(rows, 32)
    skip = first // block
    whole = pl.BlockSpec((None, block, columns), lambda i: (0, skip + i, 0))
    one_row = pl.BlockSpec((1, columns), lambda i: (0, 0))
    shape = pltpu.HBM(held[0].shape, jnp.bfloat16)
    row_shape = jax.ShapeDtypeStruct((1, columns), jnp.bfloat16)
    return pl.pallas_call(
        average_last_kernel,
        grid=(rows // block,),
        in_specs=[pl.BlockSpec(memory_space=pltpu.VMEM)] * 6
        + [pl.BlockSpec(memory_space=pl.ANY)] * 2,
        out_specs=[whole, whole, one_row, one_row],
        out_shape=[shape, shape, row_shape, row_shape],
        input_output_aliases={6: 0, 7: 1},
        compiler_params=vmem(((rows, columns), 8), ((block, columns), 4), ((8, columns), 8)),
        cost_estimate=average_cost(rows, columns),
        name="average_last",
    )(weight, far_weight, mom, far_mom, gains, far_gains, *held)


def replica_step(
    contexts,
    residual,
    cotangent,
    token_ids,
    weight,
    norm_gain,
    momentum,
    gain_momentum,
    me,
    *,
    level,
):
    distance = 1 << level
    peers = lax.axis_size("fsdp")
    tokens = contexts.shape[1]
    hidden, columns = weight.shape[1:]

    far_weight = passed_along(weight, "rep", distance)

    def from_all(block_for):
        parts = [block_for(me)]
        for shift in range(1, peers):
            parts.append(passed_along(block_for((me + shift) % peers), "fsdp", shift))
        return jnp.concatenate(parts)

    def columns_of(array):
        return lambda peer: lax.dynamic_slice_in_dim(array, peer * columns, columns, 1)

    action = token_ids[0] >= VOCAB - ACTION
    own_count = jnp.sum(action.astype(jnp.float32)).reshape(1)
    masked = jnp.where(action[:, None], cotangent[0], jnp.zeros((), cotangent.dtype))
    ctx = from_all(lambda peer: contexts[0])
    resid = from_all(columns_of(residual[0]))
    cotan = from_all(columns_of(masked))

    pre, sums = forward(own_count, ctx, weight, resid, cotan, norm_gain)
    total = sums
    for shift in range(1, peers):
        total = total + jnp.roll(passed_along(sums, "fsdp", shift), shift * tokens, 0)
    grad_pre, gains = gradient(columns * peers, pre, cotan, total, norm_gain, gain_momentum)
    far_gains = passed_along(gains, "rep", distance)

    unit = hidden // sum(SHARES)
    ctx_t = ctx.T
    first, held = 0, ()
    for share in SHARES:
        rows = share * unit
        mom = momentum_rows(ctx_t, grad_pre, momentum, first, rows, unit)
        far_mom = passed_along(mom, "rep", distance)
        if first + rows < hidden:
            held = average_rows(weight, far_weight, mom, far_mom, held, first, unit)
            first += rows
    new_weight, new_momentum, new_gain, new_gain_momentum = average_last(
        weight[0, first:], far_weight[0, first:], mom, far_mom, gains, far_gains, held, first
    )
    return new_weight, new_gain, new_momentum, new_gain_momentum


def shards(
    contexts, residual, cotangent, token_ids, step_index, weight, norm_gain, momentum, gain_momentum
):
    levels = lax.axis_size("rep").bit_length() - 1

    def branch(level):
        def run(*arrays):
            return replica_step(*arrays, level=level)

        return run

    branches = [branch(level) for level in range(levels)]
    return lax.switch(
        step_index[0] % levels,
        branches,
        contexts,
        residual,
        cotangent,
        token_ids,
        weight,
        norm_gain,
        momentum,
        gain_momentum,
        lax.axis_index("fsdp"),
    )


def solution(mesh):
    placed = (
        P("rep", "fsdp", None),
        P("rep", "fsdp", None),
        P("rep", "fsdp", None),
        P("rep", "fsdp"),
        P(),
        P("rep", None, "fsdp"),
        P("rep", "fsdp"),
        P("rep", None, "fsdp"),
        P("rep", "fsdp"),
    )
    return jax.shard_map(
        shards,
        mesh=mesh,
        in_specs=placed,
        out_specs=(
            P("rep", None, "fsdp"),
            P("rep", "fsdp"),
            P("rep", None, "fsdp"),
            P("rep", "fsdp"),
        ),
        check_vma=False,
    )
```

```python
import functools
import math

import jax
import jax.numpy as jnp
from jax import lax
from jax.experimental import pallas as pl
from jax.experimental.pallas import tpu as pltpu
from jax.sharding import PartitionSpec as P

VOCAB = 32000
ACTION = 256


EPSILON = 1e-05
BETA = 0.9
LEARN_RATE = 0.05


SHARES = (48, 12, 3, 1)
NEAR = 2
LANES = 128
TILE = 16


def passed_along(array, axis, by):
    peers = lax.axis_size(axis)
    return lax.ppermute(array, axis, [(i, (i + by) % peers) for i in range(peers)])


def cost(flops, *arrays):
    moved = sum(array.size * array.dtype.itemsize for array in arrays)
    return pl.CostEstimate(flops=flops, bytes_accessed=moved, transcendentals=0)


def vmem(*blocks):
    room = sum(2 * size * math.prod(shape) for shape, size in blocks) + 3 * 2**20
    return pltpu.CompilerParams(vmem_limit_bytes=room)


def largest_block(size, most):
    return max(block for block in range(1, most + 1) if size % block == 0)


def forward_kernel(count_ref, ctx_ref, weight_ref, resid_ref, cotan_ref, gain_ref, pre_ref, sums_ref):
    tokens, _ = resid_ref.shape
    strip = largest_block(tokens, 128)
    at = pl.program_id(0)
    lane = lax.broadcasted_iota(jnp.int32, (strip, LANES), 1)

    @pl.when(at == 0)
    def _():
        sums_ref[...] = jnp.where(
            lax.broadcasted_iota(jnp.int32, sums_ref.shape, 1) == 2, count_ref[0], 0.0
        )

    def one_strip(i, carry):
        rows = pl.ds(pl.multiple_of(i * strip, strip), strip)
        pre = resid_ref[rows, :].astype(jnp.float32) + jnp.dot(
            ctx_ref[rows, :], weight_ref[...], preferred_element_type=jnp.float32
        )
        pre_ref[rows, :] = pre
        weighted = cotan_ref[rows, :].astype(jnp.float32) * gain_ref[...].astype(jnp.float32)
        square = jnp.sum(pre * pre, axis=1, keepdims=True)
        inner = jnp.sum(weighted * pre, axis=1, keepdims=True)
        sums_ref[rows, :] += jnp.where(lane == 0, square, jnp.where(lane == 1, inner, 0.0))
        return carry

    lax.fori_loop(0, tokens // strip, one_strip, 0)


def forward(own_count, ctx, weight, resid, cotan, gain):
    tokens, columns = resid.shape
    hidden = ctx.shape[1]
    block = largest_block(columns, 256)
    out = [
        jax.ShapeDtypeStruct((tokens, columns), jnp.float32),
        jax.ShapeDtypeStruct((tokens, LANES), jnp.float32),
    ]
    by_columns = pl.BlockSpec((tokens, block), lambda i: (0, i))
    return pl.pallas_call(
        forward_kernel,
        grid=(columns // block,),
        in_specs=[
            pl.BlockSpec(memory_space=pltpu.SMEM),
            pl.BlockSpec((tokens, hidden), lambda i: (0, 0)),
            pl.BlockSpec((None, hidden, block), lambda i: (0, 0, i)),
            by_columns,
            by_columns,
            pl.BlockSpec((1, block), lambda i: (0, i)),
        ],
        out_specs=[by_columns, pl.BlockSpec((tokens, LANES), lambda i: (0, 0))],
        out_shape=out,
        compiler_params=vmem(
            ((tokens, hidden), 2), ((hidden, block), 2), ((tokens, block), 8), ((tokens, LANES), 4)
        ),
        cost_estimate=cost(2 * tokens * hidden * columns, ctx, weight, resid, cotan, *out),
        name="forward",
    )(own_count, ctx, weight, resid, cotan, gain)


def gradient_kernel(
    width, pre_ref, cotan_ref, sums_ref, gain_ref, gain_momentum_ref, grad_ref, gains_ref
):
    tokens, columns = pre_ref.shape
    gain = gain_ref[...].astype(jnp.float32)

    def one_strip(i, grad_gain):
        rows = pl.ds(pl.multiple_of(i * TILE, TILE), TILE)
        inverse = lax.rsqrt(sums_ref[rows, 0:1] / width + EPSILON)
        share = 1.0 / sums_ref[rows, 2:3]
        inner = inverse * (sums_ref[rows, 1:2] * share) / width
        normed = pre_ref[rows, :] * inverse
        scaled = cotan_ref[rows, :].astype(jnp.float32) * share
        grad = inverse * (scaled * gain - normed * inner)
        grad_ref[rows, :] = grad.astype(jnp.bfloat16)
        product = scaled * normed
        return grad_gain + (product[: TILE // 2] + product[TILE // 2 :])

    grad_gain = lax.fori_loop(
        0, tokens // TILE, one_strip, jnp.zeros((TILE // 2, columns), jnp.float32)
    )
    grad_gain = jnp.sum(grad_gain, axis=0, keepdims=True)
    mom = (BETA * gain_momentum_ref[...].astype(jnp.float32) + grad_gain).astype(jnp.bfloat16)
    mom = mom.astype(jnp.float32)
    par = (gain - LEARN_RATE * mom).astype(jnp.bfloat16).astype(jnp.float32)
    row = lax.broadcasted_iota(jnp.int32, gains_ref.shape, 0)
    gains_ref[...] = jnp.where(row == 0, par, mom).astype(jnp.bfloat16)


def gradient(width, pre, cotan, sums, gain, gain_momentum):
    tokens, columns = pre.shape
    block = largest_block(columns, 1024)
    out = [
        jax.ShapeDtypeStruct((tokens, columns), jnp.bfloat16),
        jax.ShapeDtypeStruct((2, columns), jnp.bfloat16),
    ]
    by_columns = pl.BlockSpec((tokens, block), lambda i: (0, i))
    one_row = pl.BlockSpec((1, block), lambda i: (0, i))
    return pl.pallas_call(
        functools.partial(gradient_kernel, width),
        grid=(columns // block,),
        in_specs=[
            by_columns,
            by_columns,
            pl.BlockSpec((tokens, LANES), lambda i: (0, 0)),
            one_row,
            one_row,
        ],
        out_specs=[by_columns, pl.BlockSpec((2, block), lambda i: (0, i))],
        out_shape=out,
        compiler_params=vmem(((tokens, block), 8), ((tokens, LANES), 4), ((8, block), 6)),
        cost_estimate=cost(12 * tokens * columns, pre, cotan, sums, *out),
        name="gradient",
    )(pre, cotan, sums, gain, gain_momentum)


def momentum_rows_kernel(ctx_ref, grad_ref, momentum_ref, out_ref):
    columns = momentum_ref.shape[1]
    part = largest_block(columns, 512)

    def one_part(i, carry):
        at = pl.ds(pl.multiple_of(i * part, part), part)
        grad_weight = jnp.dot(ctx_ref[...], grad_ref[:, at], preferred_element_type=jnp.float32)
        mom = BETA * momentum_ref[:, at].astype(jnp.float32) + grad_weight
        out_ref[:, at] = mom.astype(jnp.bfloat16)
        return carry

    lax.fori_loop(0, columns // part, one_part, 0)


def momentum_rows(ctx_t, grad_pre, momentum, first, rows, block):
    tokens, columns = grad_pre.shape
    skip = first // block
    return pl.pallas_call(
        momentum_rows_kernel,
        grid=(rows // block,),
        in_specs=[
            pl.BlockSpec((block, tokens), lambda i: (skip + i, 0)),
            pl.BlockSpec((tokens, columns), lambda i: (0, 0)),
            pl.BlockSpec((None, block, columns), lambda i: (0, skip + i, 0)),
        ],
        out_specs=pl.BlockSpec((block, columns), lambda i: (i, 0)),
        out_shape=jax.ShapeDtypeStruct((rows, columns), jnp.bfloat16),
        compiler_params=vmem(((block, tokens), 2), ((tokens, columns), 2), ((block, columns), 4)),
        cost_estimate=pl.CostEstimate(
            flops=2 * rows * tokens * columns,
            bytes_accessed=4 * rows * columns + 2 * tokens * (rows + columns),
            transcendentals=0,
        ),
        name="momentum_rows",
    )(ctx_t, grad_pre, momentum)


def new_parameter(old, mom):
    return (old.astype(jnp.float32) - LEARN_RATE * mom.astype(jnp.float32)).astype(jnp.bfloat16)


def average_block(
    weight_ref, far_weight_ref, mom_ref, far_mom_ref, out_weight_ref, out_mom_ref, weight_first=0
):
    rows, columns = out_weight_ref.shape
    part = largest_block(columns, 2048)
    parts = columns // part
    half = jnp.bfloat16(0.5)
    first = pl.program_id(0) * rows

    def one_part(i, carry):
        row = i // parts * TILE
        column = pl.ds(pl.multiple_of(i % parts * part, part), part)
        out = (pl.ds(pl.multiple_of(row, TILE), TILE), column)
        at = (pl.ds(pl.multiple_of(first + row, TILE), TILE), column)
        mom, far_mom = mom_ref[at], far_mom_ref[at]
        old = (pl.ds(pl.multiple_of(weight_first + row, TILE), TILE), column)
        par = new_parameter(weight_ref[old], mom) + new_parameter(far_weight_ref[old], far_mom)
        out_weight_ref[out] = par * half
        out_mom_ref[out] = (mom + far_mom) * half
        return carry

    lax.fori_loop(0, rows // TILE * parts, one_part, 0)


def average_rows_kernel(weight_ref, far_weight_ref, mom_ref, far_mom_ref, *refs):
    average_block(weight_ref, far_weight_ref, mom_ref, far_mom_ref, *refs[-2:])


def average_cost(rows, columns):
    return pl.CostEstimate(
        flops=8 * rows * columns, bytes_accessed=12 * rows * columns, transcendentals=0
    )


def average_rows(weight, far_weight, mom, far_mom, held, first, block, ready):
    rows, columns = mom.shape
    skip = first // block
    whole = pl.BlockSpec((None, block, columns), lambda i: (0, skip + i, 0))
    chunk = pl.BlockSpec(memory_space=pltpu.VMEM)
    shape = pltpu.HBM(weight.shape, jnp.bfloat16)
    return pl.pallas_call(
        average_rows_kernel,
        grid=(rows // block,),
        in_specs=[whole, whole, chunk, chunk] + [pl.BlockSpec(memory_space=pl.ANY)] * (len(held) + 1),
        out_specs=[whole, whole],
        out_shape=[shape, shape],
        input_output_aliases={4 + at: at for at in range(len(held))},
        compiler_params=vmem(((block, columns), 12)),
        cost_estimate=average_cost(rows, columns),
        name="average_rows",
    )(weight, far_weight, mom, far_mom, *held, ready)


def average_near_kernel(weight_first, *refs):
    outs = refs[8 if len(refs) == 12 else 6 :]
    first = weight_first + pl.program_id(0) * outs[0].shape[0]
    average_block(*refs[:4], *outs[:2], first)
    if len(outs) == 2:
        return
    gains_ref, far_gains_ref = refs[4:6]

    @pl.when(pl.program_id(0) == 0)
    def _():
        gains = gains_ref[...].astype(jnp.float32) + far_gains_ref[...].astype(jnp.float32)
        gains = (gains * 0.5).astype(jnp.bfloat16)
        outs[2][...] = gains[0:1]
        outs[3][...] = gains[1:2]


def average_near(weight, far_weight, mom, far_mom, held, first, weight_first, gains):
    rows, columns = mom.shape
    block = math.gcd(first, rows, 32)
    skip = first // block
    inputs = (weight, far_weight, mom, far_mom, *gains)
    whole = pl.BlockSpec((None, block, columns), lambda i: (0, skip + i, 0))
    shape = pltpu.HBM(held[0].shape, jnp.bfloat16)
    one_row = pl.BlockSpec((1, columns), lambda i: (0, 0))
    row_shape = jax.ShapeDtypeStruct((1, columns), jnp.bfloat16)
    return pl.pallas_call(
        functools.partial(average_near_kernel, weight_first),
        grid=(rows // block,),
        in_specs=[pl.BlockSpec(memory_space=pltpu.VMEM)] * len(inputs)
        + [pl.BlockSpec(memory_space=pl.ANY)] * 2,
        out_specs=[whole, whole] + [one_row for _ in gains],
        out_shape=[shape, shape] + [row_shape for _ in gains],
        input_output_aliases={len(inputs): 0, len(inputs) + 1: 1},
        compiler_params=vmem((weight.shape, 4), ((rows, columns), 4), ((block, columns), 4)),
        cost_estimate=average_cost(rows, columns),
        name="average_near",
    )(*inputs, *held)


def replica_step(
    contexts,
    residual,
    cotangent,
    token_ids,
    weight,
    norm_gain,
    momentum,
    gain_momentum,
    *,
    level,
):
    distance = 1 << level
    me, peers = lax.axis_index("fsdp"), lax.axis_size("fsdp")
    tokens = contexts.shape[1]
    hidden, columns = weight.shape[1:]

    far_weight = passed_along(weight, "rep", distance)

    def from_all(block_for):
        parts = [block_for(me)]
        for shift in range(1, peers):
            parts.append(passed_along(block_for((me + shift) % peers), "fsdp", shift))
        return jnp.concatenate(parts)

    def columns_of(array):
        return lambda peer: lax.dynamic_slice_in_dim(array, peer * columns, columns, 1)

    action = token_ids[0] >= VOCAB - ACTION
    own_count = jnp.sum(action.astype(jnp.float32)).reshape(1)
    masked = jnp.where(action[:, None], cotangent[0], jnp.zeros((), cotangent.dtype))
    ctx = from_all(lambda peer: contexts[0])
    resid = from_all(columns_of(residual[0]))
    cotan = from_all(columns_of(masked))

    pre, sums = forward(own_count, ctx, weight, resid, cotan, norm_gain)
    total = sums
    for shift in range(1, peers):
        total = total + jnp.roll(passed_along(sums, "fsdp", shift), shift * tokens, 0)
    grad_pre, gains = gradient(columns * peers, pre, cotan, total, norm_gain, gain_momentum)
    far_gains = passed_along(gains, "rep", distance)

    unit = hidden // sum(SHARES)
    ctx_t = ctx.T
    first, held = 0, ()
    near = hidden - sum(SHARES[-NEAR:]) * unit
    near_weight, far_near_weight = weight[0, near:], far_weight[0, near:]
    for share in SHARES:
        rows = share * unit
        block = math.gcd(first, rows, 128)
        mom = momentum_rows(ctx_t, grad_pre, momentum, first, rows, block)
        far_mom = passed_along(mom, "rep", distance)
        if first < near:
            held = average_rows(weight, far_weight, mom, far_mom, held, first, block, far_near_weight)
        else:
            sent = (gains, far_gains) if first + rows == hidden else ()
            held = average_near(
                near_weight, far_near_weight, mom, far_mom, held, first, first - near, sent
            )
        first += rows
    new_weight, new_momentum, new_gain, new_gain_momentum = held
    return new_weight, new_gain, new_momentum, new_gain_momentum


def shards(
    contexts, residual, cotangent, token_ids, step_index, weight, norm_gain, momentum, gain_momentum
):
    levels = lax.axis_size("rep").bit_length() - 1

    def branch(level):
        def run(*arrays):
            return replica_step(*arrays, level=level)

        return run

    branches = [branch(level) for level in range(levels)]
    return lax.switch(
        lax.rem(step_index[0], levels),
        branches,
        contexts,
        residual,
        cotangent,
        token_ids,
        weight,
        norm_gain,
        momentum,
        gain_momentum,
    )


def solution(mesh):
    placed = (
        P("rep", "fsdp", None),
        P("rep", "fsdp", None),
        P("rep", "fsdp", None),
        P("rep", "fsdp"),
        P(),
        P("rep", None, "fsdp"),
        P("rep", "fsdp"),
        P("rep", None, "fsdp"),
        P("rep", "fsdp"),
    )
    return jax.shard_map(
        shards,
        mesh=mesh,
        in_specs=placed,
        out_specs=(
            P("rep", None, "fsdp"),
            P("rep", "fsdp"),
            P("rep", None, "fsdp"),
            P("rep", "fsdp"),
        ),
        check_vma=False,
    )
```

```python
import functools
import math

import jax
import jax.numpy as jnp
from jax import lax
from jax.experimental import pallas as pl
from jax.experimental.pallas import tpu as pltpu
from jax.sharding import PartitionSpec as P

VOCAB = 32000
ACTION = 256


EPSILON = 1e-05
BETA = 0.9
LEARN_RATE = 0.05


SHARES = (24, 6, 1, 1)
NEAR = 2
LANES = 128
TILE = 16


def passed_along(array, axis, by):
    peers = lax.axis_size(axis)
    return lax.ppermute(array, axis, [(i, (i + by) % peers) for i in range(peers)])


def cost(flops, *arrays):
    moved = sum(array.size * array.dtype.itemsize for array in arrays)
    return pl.CostEstimate(flops=flops, bytes_accessed=moved, transcendentals=0)


def vmem(*blocks):
    room = sum(2 * size * math.prod(shape) for shape, size in blocks) + 3 * 2**20
    return pltpu.CompilerParams(vmem_limit_bytes=room)


def largest_block(size, most):
    return max(block for block in range(1, most + 1) if size % block == 0)


def forward_kernel(count_ref, ctx_ref, weight_ref, resid_ref, cotan_ref, gain_ref, pre_ref, sums_ref):
    tokens, _ = resid_ref.shape
    strip = largest_block(tokens, 128)
    at = pl.program_id(0)
    lane = lax.broadcasted_iota(jnp.int32, (strip, LANES), 1)

    @pl.when(at == 0)
    def _():
        sums_ref[...] = jnp.where(
            lax.broadcasted_iota(jnp.int32, sums_ref.shape, 1) == 2, count_ref[0], 0.0
        )

    def one_strip(i, carry):
        rows = pl.ds(pl.multiple_of(i * strip, strip), strip)
        pre = resid_ref[rows, :].astype(jnp.float32) + jnp.dot(
            ctx_ref[rows, :], weight_ref[...], preferred_element_type=jnp.float32
        )
        pre_ref[rows, :] = pre
        weighted = cotan_ref[rows, :].astype(jnp.float32) * gain_ref[...].astype(jnp.float32)
        square = jnp.sum(pre * pre, axis=1, keepdims=True)
        inner = jnp.sum(weighted * pre, axis=1, keepdims=True)
        sums_ref[rows, :] += jnp.where(lane == 0, square, jnp.where(lane == 1, inner, 0.0))
        return carry

    lax.fori_loop(0, tokens // strip, one_strip, 0)


def forward(own_count, ctx, weight, resid, cotan, gain):
    tokens, columns = resid.shape
    hidden = ctx.shape[1]
    block = largest_block(columns, 256)
    out = [
        jax.ShapeDtypeStruct((tokens, columns), jnp.float32),
        jax.ShapeDtypeStruct((tokens, LANES), jnp.float32),
    ]
    by_columns = pl.BlockSpec((tokens, block), lambda i: (0, i))
    return pl.pallas_call(
        forward_kernel,
        grid=(columns // block,),
        in_specs=[
            pl.BlockSpec(memory_space=pltpu.SMEM),
            pl.BlockSpec((tokens, hidden), lambda i: (0, 0)),
            pl.BlockSpec((None, hidden, block), lambda i: (0, 0, i)),
            by_columns,
            by_columns,
            pl.BlockSpec((1, block), lambda i: (0, i)),
        ],
        out_specs=[by_columns, pl.BlockSpec((tokens, LANES), lambda i: (0, 0))],
        out_shape=out,
        compiler_params=vmem(
            ((tokens, hidden), 2), ((hidden, block), 2), ((tokens, block), 8), ((tokens, LANES), 4)
        ),
        cost_estimate=cost(2 * tokens * hidden * columns, ctx, weight, resid, cotan, *out),
        name="forward",
    )(own_count, ctx, weight, resid, cotan, gain)


def gradient_kernel(
    width, pre_ref, cotan_ref, sums_ref, gain_ref, gain_momentum_ref, grad_ref, gains_ref
):
    tokens, columns = pre_ref.shape
    gain = gain_ref[...].astype(jnp.float32)

    def one_strip(i, grad_gain):
        rows = pl.ds(pl.multiple_of(i * TILE, TILE), TILE)
        inverse = lax.rsqrt(sums_ref[rows, 0:1] / width + EPSILON)
        share = 1.0 / sums_ref[rows, 2:3]
        inner = inverse * (sums_ref[rows, 1:2] * share) / width
        normed = pre_ref[rows, :] * inverse
        scaled = cotan_ref[rows, :].astype(jnp.float32) * share
        grad = inverse * (scaled * gain - normed * inner)
        grad_ref[rows, :] = grad.astype(jnp.bfloat16)
        product = scaled * normed
        return grad_gain + (product[: TILE // 2] + product[TILE // 2 :])

    grad_gain = lax.fori_loop(
        0, tokens // TILE, one_strip, jnp.zeros((TILE // 2, columns), jnp.float32)
    )
    grad_gain = jnp.sum(grad_gain, axis=0, keepdims=True)
    mom = (BETA * gain_momentum_ref[...].astype(jnp.float32) + grad_gain).astype(jnp.bfloat16)
    mom = mom.astype(jnp.float32)
    par = (gain - LEARN_RATE * mom).astype(jnp.bfloat16).astype(jnp.float32)
    row = lax.broadcasted_iota(jnp.int32, gains_ref.shape, 0)
    gains_ref[...] = jnp.where(row == 0, par, mom).astype(jnp.bfloat16)


def gradient(width, pre, cotan, sums, gain, gain_momentum):
    tokens, columns = pre.shape
    block = largest_block(columns, 1024)
    out = [
        jax.ShapeDtypeStruct((tokens, columns), jnp.bfloat16),
        jax.ShapeDtypeStruct((2, columns), jnp.bfloat16),
    ]
    by_columns = pl.BlockSpec((tokens, block), lambda i: (0, i))
    one_row = pl.BlockSpec((1, block), lambda i: (0, i))
    return pl.pallas_call(
        functools.partial(gradient_kernel, width),
        grid=(columns // block,),
        in_specs=[
            by_columns,
            by_columns,
            pl.BlockSpec((tokens, LANES), lambda i: (0, 0)),
            one_row,
            one_row,
        ],
        out_specs=[by_columns, pl.BlockSpec((2, block), lambda i: (0, i))],
        out_shape=out,
        compiler_params=vmem(((tokens, block), 8), ((tokens, LANES), 4), ((8, block), 6)),
        cost_estimate=cost(12 * tokens * columns, pre, cotan, sums, *out),
        name="gradient",
    )(pre, cotan, sums, gain, gain_momentum)


def momentum_rows_kernel(ctx_ref, grad_ref, momentum_ref, out_ref):
    columns = momentum_ref.shape[1]
    part = largest_block(columns, 512)

    def one_part(i, carry):
        at = pl.ds(pl.multiple_of(i * part, part), part)
        grad_weight = jnp.dot(ctx_ref[...], grad_ref[:, at], preferred_element_type=jnp.float32)
        mom = BETA * momentum_ref[:, at].astype(jnp.float32) + grad_weight
        out_ref[:, at] = mom.astype(jnp.bfloat16)
        return carry

    lax.fori_loop(0, columns // part, one_part, 0)


def momentum_rows(ctx_t, grad_pre, momentum, first, rows, block):
    tokens, columns = grad_pre.shape
    skip = first // block
    return pl.pallas_call(
        momentum_rows_kernel,
        grid=(rows // block,),
        in_specs=[
            pl.BlockSpec((block, tokens), lambda i: (skip + i, 0)),
            pl.BlockSpec((tokens, columns), lambda i: (0, 0)),
            pl.BlockSpec((None, block, columns), lambda i: (0, skip + i, 0)),
        ],
        out_specs=pl.BlockSpec((block, columns), lambda i: (i, 0)),
        out_shape=jax.ShapeDtypeStruct((rows, columns), jnp.bfloat16),
        compiler_params=vmem(((block, tokens), 2), ((tokens, columns), 2), ((block, columns), 4)),
        cost_estimate=pl.CostEstimate(
            flops=2 * rows * tokens * columns,
            bytes_accessed=4 * rows * columns + 2 * tokens * (rows + columns),
            transcendentals=0,
        ),
        name="momentum_rows",
    )(ctx_t, grad_pre, momentum)


def new_parameter(old, mom):
    return (old.astype(jnp.float32) - LEARN_RATE * mom.astype(jnp.float32)).astype(jnp.bfloat16)


def average_block(
    weight_ref, far_weight_ref, mom_ref, far_mom_ref, out_weight_ref, out_mom_ref, weight_first=0
):
    rows, columns = out_weight_ref.shape
    part = largest_block(columns, 2048)
    parts = columns // part
    half = jnp.bfloat16(0.5)
    first = pl.program_id(0) * rows

    def one_part(i, carry):
        row = i // parts * TILE
        column = pl.ds(pl.multiple_of(i % parts * part, part), part)
        out = (pl.ds(pl.multiple_of(row, TILE), TILE), column)
        at = (pl.ds(pl.multiple_of(first + row, TILE), TILE), column)
        mom, far_mom = mom_ref[at], far_mom_ref[at]
        old = (pl.ds(pl.multiple_of(weight_first + row, TILE), TILE), column)
        par = new_parameter(weight_ref[old], mom) + new_parameter(far_weight_ref[old], far_mom)
        out_weight_ref[out] = par * half
        out_mom_ref[out] = (mom + far_mom) * half
        return carry

    lax.fori_loop(0, rows // TILE * parts, one_part, 0)


def average_rows_kernel(weight_ref, far_weight_ref, mom_ref, far_mom_ref, *refs):
    average_block(weight_ref, far_weight_ref, mom_ref, far_mom_ref, *refs[-2:])


def average_cost(rows, columns):
    return pl.CostEstimate(
        flops=8 * rows * columns, bytes_accessed=12 * rows * columns, transcendentals=0
    )


def average_rows(weight, far_weight, mom, far_mom, held, first, block, ready):
    rows, columns = mom.shape
    skip = first // block
    whole = pl.BlockSpec((None, block, columns), lambda i: (0, skip + i, 0))
    chunk = pl.BlockSpec(memory_space=pltpu.VMEM)
    shape = pltpu.HBM(weight.shape, jnp.bfloat16)
    return pl.pallas_call(
        average_rows_kernel,
        grid=(rows // block,),
        in_specs=[whole, whole, chunk, chunk] + [pl.BlockSpec(memory_space=pl.ANY)] * (len(held) + 1),
        out_specs=[whole, whole],
        out_shape=[shape, shape],
        input_output_aliases={4 + at: at for at in range(len(held))},
        compiler_params=vmem(((block, columns), 12)),
        cost_estimate=average_cost(rows, columns),
        name="average_rows",
    )(weight, far_weight, mom, far_mom, *held, ready)


def average_near_kernel(weight_first, *refs):
    outs = refs[8 if len(refs) == 12 else 6 :]
    first = weight_first + pl.program_id(0) * outs[0].shape[0]
    average_block(*refs[:4], *outs[:2], first)
    if len(outs) == 2:
        return
    gains_ref, far_gains_ref = refs[4:6]

    @pl.when(pl.program_id(0) == 0)
    def _():
        gains = gains_ref[...].astype(jnp.float32) + far_gains_ref[...].astype(jnp.float32)
        gains = (gains * 0.5).astype(jnp.bfloat16)
        outs[2][...] = gains[0:1]
        outs[3][...] = gains[1:2]


def average_near(weight, far_weight, mom, far_mom, held, first, weight_first, gains):
    rows, columns = mom.shape
    block = math.gcd(first, rows, 16)
    skip = first // block
    inputs = (weight, far_weight, mom, far_mom, *gains)
    whole = pl.BlockSpec((None, block, columns), lambda i: (0, skip + i, 0))
    shape = pltpu.HBM(held[0].shape, jnp.bfloat16)
    one_row = pl.BlockSpec((1, columns), lambda i: (0, 0))
    row_shape = jax.ShapeDtypeStruct((1, columns), jnp.bfloat16)
    return pl.pallas_call(
        functools.partial(average_near_kernel, weight_first),
        grid=(rows // block,),
        in_specs=[pl.BlockSpec(memory_space=pltpu.VMEM)] * len(inputs)
        + [pl.BlockSpec(memory_space=pl.ANY)] * 2,
        out_specs=[whole, whole] + [one_row for _ in gains],
        out_shape=[shape, shape] + [row_shape for _ in gains],
        input_output_aliases={len(inputs): 0, len(inputs) + 1: 1},
        compiler_params=vmem((weight.shape, 4), ((rows, columns), 4), ((block, columns), 4)),
        cost_estimate=average_cost(rows, columns),
        name="average_near",
    )(*inputs, *held)


def replica_step(
    contexts,
    residual,
    cotangent,
    token_ids,
    weight,
    norm_gain,
    momentum,
    gain_momentum,
    me,
    *,
    level,
):
    distance = 1 << level
    peers = lax.axis_size("fsdp")
    tokens = contexts.shape[1]
    hidden, columns = weight.shape[1:]

    far_weight = passed_along(weight, "rep", distance)

    def from_all(block_for):
        parts = [block_for(me)]
        for shift in range(1, peers):
            parts.append(passed_along(block_for((me + shift) % peers), "fsdp", shift))
        return jnp.concatenate(parts)

    def columns_of(array):
        return lambda peer: lax.dynamic_slice_in_dim(array, peer * columns, columns, 1)

    action = token_ids[0] >= VOCAB - ACTION
    own_count = jnp.sum(action.astype(jnp.float32)).reshape(1)
    masked = jnp.where(action[:, None], cotangent[0], jnp.zeros((), cotangent.dtype))
    ctx = from_all(lambda peer: contexts[0])
    resid = from_all(columns_of(residual[0]))
    cotan = from_all(columns_of(masked))

    pre, sums = forward(own_count, ctx, weight, resid, cotan, norm_gain)
    total = sums
    for shift in range(1, peers):
        total = total + jnp.roll(passed_along(sums, "fsdp", shift), shift * tokens, 0)
    grad_pre, gains = gradient(columns * peers, pre, cotan, total, norm_gain, gain_momentum)
    far_gains = passed_along(gains, "rep", distance)

    unit = hidden // sum(SHARES)
    ctx_t = ctx.T
    first, held = 0, ()
    near = hidden - sum(SHARES[-NEAR:]) * unit
    near_weight, far_near_weight = weight[0, near:], far_weight[0, near:]
    for share in SHARES:
        rows = share * unit
        block = math.gcd(first, rows, 128)
        mom = momentum_rows(ctx_t, grad_pre, momentum, first, rows, block)
        far_mom = passed_along(mom, "rep", distance)
        if first < near:
            held = average_rows(weight, far_weight, mom, far_mom, held, first, block, far_near_weight)
        else:
            sent = (gains, far_gains) if first + rows == hidden else ()
            held = average_near(
                near_weight, far_near_weight, mom, far_mom, held, first, first - near, sent
            )
        first += rows
    new_weight, new_momentum, new_gain, new_gain_momentum = held
    return new_weight, new_gain, new_momentum, new_gain_momentum


def shards(
    contexts, residual, cotangent, token_ids, step_index, weight, norm_gain, momentum, gain_momentum
):
    levels = lax.axis_size("rep").bit_length() - 1

    def branch(level):
        def run(*arrays):
            return replica_step(*arrays, level=level)

        return run

    branches = [branch(level) for level in range(levels)]
    return lax.switch(
        step_index[0] % levels,
        branches,
        contexts,
        residual,
        cotangent,
        token_ids,
        weight,
        norm_gain,
        momentum,
        gain_momentum,
        lax.axis_index("fsdp"),
    )


def solution(mesh):
    placed = (
        P("rep", "fsdp", None),
        P("rep", "fsdp", None),
        P("rep", "fsdp", None),
        P("rep", "fsdp"),
        P(),
        P("rep", None, "fsdp"),
        P("rep", "fsdp"),
        P("rep", None, "fsdp"),
        P("rep", "fsdp"),
    )
    return jax.shard_map(
        shards,
        mesh=mesh,
        in_specs=placed,
        out_specs=(
            P("rep", None, "fsdp"),
            P("rep", "fsdp"),
            P("rep", None, "fsdp"),
            P("rep", "fsdp"),
        ),
        check_vma=False,
    )
```
